512 devices in a mesh: seq: 32 (over x, z_hi, core), team: 16 (over z_lo, y).
Axes of the slice: x: 4, y: 8, z: 8 (z_hi: 4, z_lo: 2; z = z_hi * 2 + z_lo), core: 2. Of those that a mesh axis runs over, the one named last changes fastest.
Arguments:
- tokens: bfloat16 [32768, 1024], P(('seq', 'team')), may hold values from -6 to 6
- norm_gain: float32 [1024], replicated, may hold values from 0.1 to 1.9
- w_qkv: bfloat16 [1024, 3072], P('team'), may hold values from -1 to 1
- block_lists: int32 [256, 8], P('seq'), may hold values from 0 to 255, as said below
- block_counts: int32 [256], P('seq'), may hold values from 1 to 8, as said below
Outputs:
- attended: bfloat16 [32768, 1024], P('seq', 'team')
The draws below stay inside these ranges and needn't reach their ends.
Inputs may be any that keep to these rules, and one draw needn't show every extreme that they name: `block_lists`: each query tile's list holds 8 distinct key tiles; the first is the query tile itself, the others are tiles of other sequence shards (a shard holds 8 tiles). The lists of one shard's query tiles name at most 2 distinct tiles of any one other shard, and exactly 2 of at least one other shard. `block_counts`: the first query tile has 1 valid entry and the last has 8.
All inputs are finite; a program needn't handle non-finite values.
Results may differ from the reference program's by a relative error of at most 0.0083.
Values may be sent and summed in bfloat16 or wider, within the bound.
A program may use at most 64 MiB of HBM per device.

```python
import jax
import jax.numpy as jnp
from jax import lax

D = 1024
HEADS = 16
HD = 64
TILE = 128
MAXB = 8
CAP = 2
SEQ_DEV = 1024
TOKENS = 32768
TILES = 256


def draw_tokens(key, part):
    noise_key = jax.random.fold_in(key, 17)
    values = jax.random.truncated_normal(noise_key, -6.0, 6.0, (TOKENS, D), jnp.float32)
    return values.astype(jnp.bfloat16)


def draw_w_qkv(key, part):
    noise_key = jax.random.fold_in(key, 29)
    values = jax.random.truncated_normal(noise_key, -6.0, 6.0, (D, 3 * D), jnp.float32) * D ** (-0.5)
    return values.astype(jnp.bfloat16)


def draw_block_lists(key, part):
    shard_tiles = SEQ_DEV // TILE
    shards = TILES // shard_tiles
    others = MAXB - 1
    candidates = (shards - 1) * CAP
    reach = min(candidates, shard_tiles * others)

    def one_shard(shard, shard_key):
        first, second, third, fourth = jax.random.split(shard_key, 4)
        local_picks = jax.vmap(lambda k: jax.random.permutation(k, shard_tiles)[:CAP])(jax.random.split(first, shards - 1)).astype(jnp.int32)
        shuffled = jax.random.permutation(second, candidates).astype(jnp.int32)
        position = jnp.argsort(shuffled).astype(jnp.int32)
        favored = jax.random.randint(third, (), 0, shards - 1).astype(jnp.int32)
        early = jax.random.permutation(fourth, reach - CAP + 1)[:CAP].astype(jnp.int32)
        every = jnp.arange(candidates, dtype=jnp.int32)
        sort_keys = jnp.where(every // CAP == favored, 2 * early[every % CAP], 2 * position + 1)
        ranked = jnp.argsort(sort_keys).astype(jnp.int32)
        slot_ids = jnp.arange(shard_tiles * others, dtype=jnp.int32) % candidates
        picked = ranked[slot_ids]
        owner = (shard + 1 + picked // CAP) % shards
        tile_ids = owner * shard_tiles + local_picks[picked // CAP, picked % CAP]
        own_ids = shard * shard_tiles + jnp.arange(shard_tiles, dtype=jnp.int32)
        return jnp.concatenate([own_ids[:, None], tile_ids.reshape(shard_tiles, others)], axis=1).astype(jnp.int32)
    result = jax.vmap(one_shard)(jnp.arange(shards, dtype=jnp.int32), jax.random.split(key, shards))
    return result.reshape(TILES, MAXB).astype(jnp.int32)


def draw_block_counts(key, part):
    rows = jnp.arange(TILES, dtype=jnp.int32)
    tops = 1 + (MAXB - 1) * (rows + 1) // TILES
    counts = jax.random.randint(key, (TILES,), 1, tops + 1).astype(jnp.int32)
    return counts.at[TILES - 1].set(MAXB).astype(jnp.int32)


def setup_inputs(seed: int = 0) -> dict:
    streams_of = jax.random.split(jax.random.key(seed), 6)
    return {
        "tokens": draw_tokens(jax.random.fold_in(streams_of[5], 71), 0),
        "norm_gain": jnp.clip(1.0 + 0.18 * jax.random.normal(streams_of[1], (D,), jnp.float32), 0.1, 1.9),
        "w_qkv": draw_w_qkv(jax.random.fold_in(streams_of[5], 71), 0),
        "block_lists": draw_block_lists(jax.random.fold_in(streams_of[5], 71), 0),
        "block_counts": draw_block_counts(jax.random.fold_in(streams_of[5], 71), 0),
    }


def reference(tokens, norm_gain, w_qkv, block_lists, block_counts):
    xf = tokens.astype(jnp.float32)
    normed = (xf * lax.rsqrt(lax.optimization_barrier(jnp.mean(xf * xf, axis=-1, keepdims=True)) + 1e-05) * norm_gain).astype(jnp.bfloat16)
    qkv = jnp.dot(normed, w_qkv, preferred_element_type=jnp.float32).astype(jnp.bfloat16)
    qkv = qkv.reshape(TOKENS, HEADS, 3 * HD)
    query = qkv[:, :, :HD]
    keys = qkv[:, :, HD:2 * HD]
    values = qkv[:, :, 2 * HD:]
    offsets = jnp.arange(TILE, dtype=jnp.int32)

    def one_tile(args):
        index, listed, count = args
        rows = lax.dynamic_slice_in_dim(query, (index * TILE).astype(jnp.int32), TILE, 0)
        picks = (listed[:, None] * TILE + offsets[None, :]).reshape(-1).astype(jnp.int32)
        kgot = keys[picks].astype(jnp.float32)
        vgot = values[picks].astype(jnp.float32)
        scores = jnp.einsum('qhd,khd->hqk', rows.astype(jnp.float32), kgot) * HD ** (-0.5)
        valid = jnp.repeat(jnp.arange(MAXB, dtype=jnp.int32) < count, TILE)
        masked = jnp.where(valid[None, None, :], scores, -1e+30)
        top = lax.optimization_barrier(jnp.max(masked, axis=-1, keepdims=True))
        weights = jnp.where(valid[None, None, :], jnp.exp(masked - top), 0.0)
        total = lax.optimization_barrier(jnp.sum(weights, axis=-1))
        rounded = weights.astype(jnp.bfloat16).astype(jnp.float32)
        summed = jnp.einsum('hqk,khd->hqd', rounded, vgot) / total[:, :, None]
        return jnp.transpose(summed, (1, 0, 2)).reshape(TILE, D).astype(jnp.bfloat16)
    result = lax.map(one_tile, (jnp.arange(TILES, dtype=jnp.int32), block_lists, block_counts))
    return result.reshape(TOKENS, D)
```

```python
import functools

import jax
import jax.numpy as jnp
from jax import lax
from jax.experimental import pallas as pl
from jax.experimental.pallas import tpu as pltpu
from jax.sharding import PartitionSpec as P

HEADS = 16
HD = 64
TILE = 128
MAXB = 8


def attend_kernel(lists, counts, q_ref, kv_hbm, out_ref, kv, sems):
    tiles = q_ref.shape[0] // TILE

    def fetch(i, j):
        return pltpu.make_async_copy(kv_hbm.at[lists[i, j]], kv.at[i, pl.ds(j * TILE, TILE)], sems.at[i])

    for i in range(tiles):
        for j in range(MAXB):
            fetch(i, j).start()

    column = lax.broadcasted_iota(jnp.int32, (TILE, MAXB * TILE), 1)

    def one_tile(i, carry):
        for j in range(MAXB):
            fetch(i, j).wait()
        rows = pl.ds(pl.multiple_of(i * TILE, TILE), TILE)
        keys = kv[i]
        scores = lax.dot_general(
            q_ref[rows, :], keys, (((1,), (1,)), ((), ())), preferred_element_type=jnp.float32
        )
        scores = jnp.where(column < counts[i] * TILE, scores * HD ** (-0.5), -1e30)
        top = jnp.max(scores, axis=-1, keepdims=True)
        weights = jnp.exp(scores - top)
        total = jnp.sum(weights, axis=-1, keepdims=True)
        summed = jnp.dot(weights.astype(jnp.bfloat16), keys, preferred_element_type=jnp.float32)
        out_ref[rows, :] = (summed / total)[:, HD:].astype(jnp.bfloat16)
        return carry

    lax.fori_loop(0, tiles, one_tile, 0)


def attend(lists, counts, q, kv):
    rows = q.shape[0]
    tiles = rows // TILE
    return pl.pallas_call(
        attend_kernel,
        grid_spec=pltpu.PrefetchScalarGridSpec(
            num_scalar_prefetch=2,
            grid=(1,),
            in_specs=[
                pl.BlockSpec((rows, 2 * HD), lambda i, *_: (0, 0)),
                pl.BlockSpec(memory_space=pl.ANY),
            ],
            out_specs=pl.BlockSpec((rows, HD), lambda i, *_: (0, 0)),
            scratch_shapes=[
                pltpu.VMEM((tiles, MAXB * TILE, 2 * HD), jnp.bfloat16),
                pltpu.SemaphoreType.DMA((tiles,)),
            ],
        ),
        out_shape=jax.ShapeDtypeStruct((rows, HD), jnp.bfloat16),
        name="attend",
    )(lists, counts, q, kv)


def on_device(tokens, norm_gain, w_qkv, block_lists, block_counts):
    xf = tokens.astype(jnp.float32)
    normed = (xf * lax.rsqrt(jnp.mean(xf * xf, axis=-1, keepdims=True) + 1e-05) * norm_gain).astype(
        jnp.bfloat16
    )
    depth = w_qkv.shape[0]
    w_head = lax.all_to_all(
        w_qkv.reshape(depth, HEADS, 3 * HD), "team", split_axis=1, concat_axis=0, tiled=True
    ).reshape(-1, 3 * HD)
    rows = lax.all_gather(normed, "team", axis=0, tiled=True)
    qkv = jnp.dot(rows, w_head, preferred_element_type=jnp.float32).astype(jnp.bfloat16)
    q = jnp.pad(qkv[:, :HD], ((0, 0), (0, HD)))
    kv = lax.all_gather(qkv[:, HD:], "seq", axis=0, tiled=True)
    return attend(block_lists, block_counts, q, kv.reshape(-1, TILE, 2 * HD))


def solution(mesh):
    in_specs = (P(("seq", "team"), None), P(), P("team", None), P("seq", None), P("seq"))
    out_specs = P("seq", "team")
    return jax.shard_map(
        on_device, mesh=mesh, in_specs=in_specs, out_specs=out_specs, check_vma=False
    )
```

```python
import jax
import jax.numpy as jnp
from jax import lax
from jax.experimental import pallas as pl
from jax.experimental.pallas import tpu as pltpu
from jax.sharding import PartitionSpec as P

HEADS = 16
HD = 64
TILE = 128
MAXB = 8
RING = 8
MESH = pl.DeviceIdType.MESH
TEAM_SPACE = pltpu.VMEM
SEQ_SPACE = pl.ANY

def meet(peers):
    barrier = pltpu.get_barrier_semaphore()
    for peer in peers:
        pl.semaphore_signal(barrier, inc=1, device_id=peer, device_id_type=MESH)
    pl.semaphore_wait(barrier, len(peers))


def team_kernel(x_ref, w_ref, out, w_out, local_sem, send_sem, recv_sem, w_send_sem, w_recv_sem):
    me = lax.axis_index("team")
    z, y = me // RING, lax.rem(me, RING)
    other = 1 - z

    def slot(plane, shift):
        return plane * RING + lax.rem(y + RING + shift, RING)

    right, left, across = {"team": slot(z, 1)}, {"team": slot(z, -1)}, {"team": slot(other, 0)}
    sent = []

    def send(src, index, to, arrival):
        copy = pltpu.make_async_remote_copy(
            src_ref=src,
            dst_ref=out.at[index],
            send_sem=send_sem.at[len(sent)],
            recv_sem=recv_sem.at[arrival],
            device_id=to,
            device_id_type=MESH,
        )
        copy.start()
        sent.append(copy)

    def arrived(index, arrival):
        pltpu.make_async_remote_copy(
            src_ref=x_ref,
            dst_ref=out.at[index],
            send_sem=send_sem.at[0],
            recv_sem=recv_sem.at[arrival],
            device_id=right,
            device_id_type=MESH,
        ).wait_recv()

    def w_copy(k):
        peer = lax.rem(me + k, HEADS)
        return pltpu.make_async_remote_copy(
            src_ref=w_ref.at[peer],
            dst_ref=w_out.at[me],
            send_sem=w_send_sem.at[k],
            recv_sem=w_recv_sem.at[k],
            device_id={"team": peer},
            device_id_type=MESH,
        )

    own = pltpu.make_async_copy(x_ref, out.at[me], local_sem.at[0])
    own.start()
    own_w = pltpu.make_async_copy(w_ref.at[me], w_out.at[me], local_sem.at[1])
    own_w.start()
    meet([{"team": lax.rem(me + k, HEADS)} for k in range(1, HEADS)])

    send(x_ref, me, right, 0)
    send(x_ref, me, left, 4)
    send(x_ref, me, across, 7)
    for k in range(1, HEADS):
        w_copy(k).start()
    arrived(slot(other, 0), 7)
    send(out.at[slot(other, 0)], slot(other, 0), right, 8)
    send(out.at[slot(other, 0)], slot(other, 0), left, 10)
    for d in (1, 2, 3):
        arrived(slot(z, -d), d - 1)
        send(out.at[slot(z, -d)], slot(z, -d), right, d)
        if d == 3:
            send(out.at[slot(z, -3)], slot(z, -3), across, 12)
        arrived(slot(z, d), 3 + d)
        if d < 3:
            send(out.at[slot(z, d)], slot(z, d), left, 4 + d)
            arrived(slot(other, -d), 7 + d)
            arrived(slot(other, d), 9 + d)
            if d == 1:
                send(out.at[slot(other, -1)], slot(other, -1), right, 9)
                send(out.at[slot(other, 1)], slot(other, 1), left, 11)
        else:
            send(out.at[slot(z, 3)], slot(z, 3), across, 14)
    arrived(slot(z, -4), 3)
    send(out.at[slot(z, -4)], slot(z, -4), across, 13)
    arrived(slot(other, -3), 12)
    arrived(slot(other, 3), 14)
    arrived(slot(other, -4), 13)
    for k in range(1, HEADS):
        peer = lax.rem(me + HEADS - k, HEADS)
        pltpu.make_async_remote_copy(
            src_ref=w_ref.at[peer],
            dst_ref=w_out.at[peer],
            send_sem=w_send_sem.at[k],
            recv_sem=w_recv_sem.at[k],
            device_id={"team": peer},
            device_id_type=MESH,
        ).wait_recv()
    for k in range(1, HEADS):
        w_copy(k).wait_send()
    for copy in sent:
        copy.wait_send()
    own.wait()
    own_w.wait()


def team_gather(normed, w):
    return pl.pallas_call(
        team_kernel,
        in_specs=[pl.BlockSpec(memory_space=TEAM_SPACE)] * 2,
        out_specs=[pl.BlockSpec(memory_space=TEAM_SPACE)] * 2,
        out_shape=[
            jax.ShapeDtypeStruct((HEADS,) + normed.shape, normed.dtype),
            jax.ShapeDtypeStruct(w.shape, w.dtype),
        ],
        scratch_shapes=[
            pltpu.SemaphoreType.DMA((2,)),
            pltpu.SemaphoreType.DMA((15,)),
            pltpu.SemaphoreType.DMA((15,)),
            pltpu.SemaphoreType.DMA((HEADS,)),
            pltpu.SemaphoreType.DMA((HEADS,)),
        ],
        compiler_params=pltpu.CompilerParams(collective_id=0, has_side_effects=True),
        name="team_gather",
    )(normed, w)


def seq_kernel(kv_ref, out, local_sem, send_sem, z_sem, x_sem, pair_sem):
    me = lax.axis_index("seq")
    x, z, core = me // 8, lax.rem(me // 2, 4), lax.rem(me, 2)
    half = kv_ref.shape[0] // 2
    shifts = (0, -1, 1, 2)

    def place(xs, zs, c):
        return lax.rem(x + 4 + xs, 4) * 8 + lax.rem(z + 4 + zs, 4) * 2 + c

    z_up, z_down = {"seq": place(0, 1, core)}, {"seq": place(0, -1, core)}
    x_up, x_down = {"seq": place(1, 0, core)}, {"seq": place(-1, 0, core)}
    pair = {"seq": place(0, 0, 1 - core)}
    parts = {"all": pl.ds(0, 2 * half), "low": pl.ds(0, half), "high": pl.ds(half, half)}
    sent = []

    def describe(index, part, to, arrival, send_index, first):
        src = kv_ref if first else out.at[index]
        return pltpu.make_async_remote_copy(
            src_ref=src.at[parts[part]],
            dst_ref=out.at[index, parts[part]],
            send_sem=send_sem.at[send_index],
            recv_sem=arrival,
            device_id=to,
            device_id_type=MESH,
        )

    def send(index, part, to, arrival, first=False):
        copy = describe(index, part, to, arrival, len(sent), first)
        copy.start()
        sent.append(copy)

    def arrived(index, part, arrival):
        describe(index, part, pair, arrival, 0, True).wait_recv()

    def spread(zi):
        index = place(0, shifts[zi], core)
        first = zi == 0
        send(index, "all", x_up, x_sem.at[4 * zi], first)
        send(index, "all", x_down, x_sem.at[4 * zi + 1], first)
        send(index, "all", pair, pair_sem.at[4 * zi], first)

    def relay(zi):
        below, above = place(-1, shifts[zi], core), place(1, shifts[zi], core)
        arrived(below, "all", x_sem.at[4 * zi])
        send(below, "low", x_up, x_sem.at[4 * zi + 2])
        send(below, "all", pair, pair_sem.at[4 * zi + 1])
        arrived(above, "all", x_sem.at[4 * zi + 1])
        send(above, "high", x_down, x_sem.at[4 * zi + 3])
        send(above, "all", pair, pair_sem.at[4 * zi + 2])

    def finish(zi):
        far = place(2, shifts[zi], core)
        arrived(far, "low", x_sem.at[4 * zi + 2])
        arrived(far, "high", x_sem.at[4 * zi + 3])
        send(far, "all", pair, pair_sem.at[4 * zi + 3])

    own = pltpu.make_async_copy(kv_ref, out.at[me], local_sem)
    own.start()
    meet([z_up, z_down, x_up, x_down, pair])
    send(me, "all", z_up, z_sem.at[0], True)
    send(me, "all", z_down, z_sem.at[1], True)
    spread(0)
    relay(0)
    arrived(place(0, -1, core), "all", z_sem.at[0])
    send(place(0, -1, core), "low", z_up, z_sem.at[2])
    spread(1)
    arrived(place(0, 1, core), "all", z_sem.at[1])
    send(place(0, 1, core), "high", z_down, z_sem.at[3])
    spread(2)
    finish(0)
    relay(1)
    arrived(place(0, 2, core), "low", z_sem.at[2])
    arrived(place(0, 2, core), "high", z_sem.at[3])
    spread(3)
    relay(2)
    finish(1)
    finish(2)
    relay(3)
    finish(3)
    for zi in range(4):
        for xi in range(4):
            arrived(place(shifts[xi], shifts[zi], 1 - core), "all", pair_sem.at[4 * zi + xi])
    for copy in sent:
        copy.wait_send()
    own.wait()


def seq_gather(kv):
    return pl.pallas_call(
        seq_kernel,
        in_specs=[pl.BlockSpec(memory_space=SEQ_SPACE)],
        out_specs=pl.BlockSpec(memory_space=SEQ_SPACE),
        out_shape=jax.ShapeDtypeStruct((32,) + kv.shape, kv.dtype),
        scratch_shapes=[
            pltpu.SemaphoreType.DMA,
            pltpu.SemaphoreType.DMA((36,)),
            pltpu.SemaphoreType.DMA((4,)),
            pltpu.SemaphoreType.DMA((16,)),
            pltpu.SemaphoreType.DMA((16,)),
        ],
        compiler_params=pltpu.CompilerParams(collective_id=1, has_side_effects=True),
        name="seq_gather",
    )(kv)


def attend_kernel(lists, counts, q_ref, kv_hbm, out_ref, kv, sems):
    tiles = q_ref.shape[0] // TILE

    def fetch(i, j):
        return pltpu.make_async_copy(kv_hbm.at[lists[i, j]], kv.at[i, pl.ds(j * TILE, TILE)], sems.at[i])

    for i in range(tiles):
        for j in range(MAXB):
            fetch(i, j).start()

    column = lax.broadcasted_iota(jnp.int32, (TILE, MAXB * TILE), 1)

    def one_tile(i, carry):
        for j in range(MAXB):
            fetch(i, j).wait()
        rows = pl.ds(pl.multiple_of(i * TILE, TILE), TILE)
        keys = kv[i]
        scores = lax.dot_general(
            q_ref[rows, :], keys, (((1,), (1,)), ((), ())), preferred_element_type=jnp.float32
        )
        scores = jnp.where(column < counts[i] * TILE, scores * HD ** (-0.5), -1e30)
        top = jnp.max(scores, axis=-1, keepdims=True)
        weights = jnp.exp(scores - top)
        total = jnp.sum(weights, axis=-1, keepdims=True)
        summed = jnp.dot(weights.astype(jnp.bfloat16), keys, preferred_element_type=jnp.float32)
        out_ref[rows, :] = (summed / total)[:, HD:].astype(jnp.bfloat16)
        return carry

    lax.fori_loop(0, tiles, one_tile, 0)


def attend(lists, counts, q, kv):
    rows = q.shape[0]
    tiles = rows // TILE
    return pl.pallas_call(
        attend_kernel,
        grid_spec=pltpu.PrefetchScalarGridSpec(
            num_scalar_prefetch=2,
            grid=(1,),
            in_specs=[
                pl.BlockSpec((rows, 2 * HD), lambda i, *_: (0, 0)),
                pl.BlockSpec(memory_space=pl.ANY),
            ],
            out_specs=pl.BlockSpec((rows, HD), lambda i, *_: (0, 0)),
            scratch_shapes=[
                pltpu.VMEM((tiles, MAXB * TILE, 2 * HD), jnp.bfloat16),
                pltpu.SemaphoreType.DMA((tiles,)),
            ],
        ),
        out_shape=jax.ShapeDtypeStruct((rows, HD), jnp.bfloat16),
        name="attend",
    )(lists, counts, q, kv)


def on_device(tokens, norm_gain, w_qkv, block_lists, block_counts):
    xf = tokens.astype(jnp.float32)
    normed = (xf * lax.rsqrt(jnp.mean(xf * xf, axis=-1, keepdims=True) + 1e-05) * norm_gain).astype(
        jnp.bfloat16
    )
    depth = w_qkv.shape[0]
    w_blocks = w_qkv.reshape(depth, HEADS, 3 * HD).transpose(1, 0, 2)
    rows, w_head = team_gather(normed, w_blocks)
    rows, w_head = rows.reshape(-1, rows.shape[-1]), w_head.reshape(-1, 3 * HD)
    qkv = jnp.dot(rows, w_head, preferred_element_type=jnp.float32).astype(jnp.bfloat16)
    q = jnp.pad(qkv[:, :HD], ((0, 0), (0, HD)))
    kv = seq_gather(qkv[:, HD:])
    return attend(block_lists, block_counts, q, kv.reshape(-1, TILE, 2 * HD))


def solution(mesh):
    in_specs = (P(("seq", "team"), None), P(), P("team", None), P("seq", None), P("seq"))
    out_specs = P("seq", "team")
    return jax.shard_map(
        on_device, mesh=mesh, in_specs=in_specs, out_specs=out_specs, check_vma=False
    )
```

```python
import jax
import jax.numpy as jnp
from jax import lax
from jax.experimental import pallas as pl
from jax.experimental.pallas import tpu as pltpu
from jax.sharding import PartitionSpec as P

HEADS = 16
HD = 64
TILE = 128
MAXB = 8
RING = 8
WINDOW = 256
MESH = pl.DeviceIdType.MESH
TEAM_SPACE = pltpu.VMEM
SEQ_SPACE = pl.ANY

def meet(peers):
    barrier = pltpu.get_barrier_semaphore()
    for peer in peers:
        pl.semaphore_signal(barrier, inc=1, device_id=peer, device_id_type=MESH)
    pl.semaphore_wait(barrier, len(peers))


def team_kernel(
    x_ref, w_ref, out, w_out, local_sem, send_sem, recv_sem, w_send_sem, w_recv_sem, p_send_sem, p_recv_sem
):
    me = lax.axis_index("team")
    z, y = me // RING, lax.rem(me, RING)
    other = 1 - z
    shard = lax.axis_index("seq")
    core = lax.rem(shard, 2)
    pair = {"seq": shard + 1 - 2 * core}
    depth = w_ref.shape[0]
    half = depth // 2
    mine = pl.ds(pl.multiple_of(core * half, half), half)
    theirs = pl.ds(pl.multiple_of((1 - core) * half, half), half)

    def window(head):
        return pl.ds(pl.multiple_of((3 * head) // 2 * 128, 128), WINDOW)

    def slot(plane, shift):
        return plane * RING + lax.rem(y + RING + shift, RING)

    right, left, across = {"team": slot(z, 1)}, {"team": slot(z, -1)}, {"team": slot(other, 0)}
    sent = []

    def send(src, index, to, arrival):
        copy = pltpu.make_async_remote_copy(
            src_ref=src,
            dst_ref=out.at[index],
            send_sem=send_sem.at[len(sent)],
            recv_sem=recv_sem.at[arrival],
            device_id=to,
            device_id_type=MESH,
        )
        copy.start()
        sent.append(copy)

    def arrived(index, arrival):
        pltpu.make_async_remote_copy(
            src_ref=x_ref,
            dst_ref=out.at[index],
            send_sem=send_sem.at[0],
            recv_sem=recv_sem.at[arrival],
            device_id=right,
            device_id_type=MESH,
        ).wait_recv()

    def w_copy(k):
        peer = lax.rem(me + k, HEADS)
        return pltpu.make_async_remote_copy(
            src_ref=w_ref.at[mine, window(peer)],
            dst_ref=w_out.at[me, mine],
            send_sem=w_send_sem.at[k],
            recv_sem=w_recv_sem.at[k],
            device_id={"team": peer},
            device_id_type=MESH,
        )

    def w_arrived(k):
        peer = lax.rem(me + HEADS - k, HEADS)
        pltpu.make_async_remote_copy(
            src_ref=w_ref.at[mine, window(peer)],
            dst_ref=w_out.at[peer, mine],
            send_sem=w_send_sem.at[k],
            recv_sem=w_recv_sem.at[k],
            device_id={"team": peer},
            device_id_type=MESH,
        ).wait_recv()

    def w_pass(k, rows):
        peer = lax.rem(me + HEADS - k, HEADS)
        return pltpu.make_async_remote_copy(
            src_ref=w_out.at[peer, rows],
            dst_ref=w_out.at[peer, rows],
            send_sem=p_send_sem.at[k],
            recv_sem=p_recv_sem.at[k],
            device_id=pair,
            device_id_type=MESH,
        )

    own = pltpu.make_async_copy(x_ref, out.at[me], local_sem.at[0])
    own.start()
    own_w = pltpu.make_async_copy(w_ref.at[:, window(me)], w_out.at[me], local_sem.at[1])
    own_w.start()
    meet([{"team": lax.rem(me + k, HEADS)} for k in range(1, HEADS)] + [pair])

    send(x_ref, me, right, 0)
    send(x_ref, me, left, 4)
    send(x_ref, me, across, 7)
    for k in range(1, HEADS):
        w_copy(k).start()
    arrived(slot(other, 0), 7)
    send(out.at[slot(other, 0)], slot(other, 0), right, 8)
    send(out.at[slot(other, 0)], slot(other, 0), left, 10)
    for d in (1, 2, 3):
        arrived(slot(z, -d), d - 1)
        send(out.at[slot(z, -d)], slot(z, -d), right, d)
        if d == 3:
            send(out.at[slot(z, -3)], slot(z, -3), across, 12)
        arrived(slot(z, d), 3 + d)
        if d < 3:
            send(out.at[slot(z, d)], slot(z, d), left, 4 + d)
            arrived(slot(other, -d), 7 + d)
            arrived(slot(other, d), 9 + d)
            if d == 1:
                send(out.at[slot(other, -1)], slot(other, -1), right, 9)
                send(out.at[slot(other, 1)], slot(other, 1), left, 11)
        else:
            send(out.at[slot(z, 3)], slot(z, 3), across, 14)
    arrived(slot(z, -4), 3)
    send(out.at[slot(z, -4)], slot(z, -4), across, 13)
    for k in range(1, HEADS):
        w_arrived(k)
        w_pass(k, mine).start()
    arrived(slot(other, -3), 12)
    arrived(slot(other, 3), 14)
    arrived(slot(other, -4), 13)
    for k in range(1, HEADS):
        w_pass(k, theirs).wait_recv()
    for k in range(1, HEADS):
        w_copy(k).wait_send()
        w_pass(k, mine).wait_send()
    for copy in sent:
        copy.wait_send()
    own.wait()
    own_w.wait()


def team_gather(normed, w):
    return pl.pallas_call(
        team_kernel,
        in_specs=[pl.BlockSpec(memory_space=TEAM_SPACE)] * 2,
        out_specs=[pl.BlockSpec(memory_space=TEAM_SPACE)] * 2,
        out_shape=[
            jax.ShapeDtypeStruct((HEADS,) + normed.shape, normed.dtype),
            jax.ShapeDtypeStruct((HEADS, w.shape[0], WINDOW), w.dtype),
        ],
        scratch_shapes=[
            pltpu.SemaphoreType.DMA((2,)),
            pltpu.SemaphoreType.DMA((15,)),
            pltpu.SemaphoreType.DMA((15,)),
            pltpu.SemaphoreType.DMA((HEADS,)),
            pltpu.SemaphoreType.DMA((HEADS,)),
            pltpu.SemaphoreType.DMA((HEADS,)),
            pltpu.SemaphoreType.DMA((HEADS,)),
        ],
        compiler_params=pltpu.CompilerParams(collective_id=0, has_side_effects=True),
        name="team_gather",
    )(normed, w)


def seq_kernel(kv_ref, out, local_sem, send_sem, z_sem, x_sem, pair_sem):
    me = lax.axis_index("seq")
    x, z, core = me // 8, lax.rem(me // 2, 4), lax.rem(me, 2)
    half = kv_ref.shape[0] // 2
    shifts = (0, -1, 1, 2)

    def place(xs, zs, c):
        return lax.rem(x + 4 + xs, 4) * 8 + lax.rem(z + 4 + zs, 4) * 2 + c

    z_up, z_down = {"seq": place(0, 1, core)}, {"seq": place(0, -1, core)}
    x_up, x_down = {"seq": place(1, 0, core)}, {"seq": place(-1, 0, core)}
    pair = {"seq": place(0, 0, 1 - core)}
    parts = {"all": pl.ds(0, 2 * half), "low": pl.ds(0, half), "high": pl.ds(half, half)}
    sent = []

    def describe(index, part, to, arrival, send_index, first):
        src = kv_ref if first else out.at[index]
        return pltpu.make_async_remote_copy(
            src_ref=src.at[parts[part]],
            dst_ref=out.at[index, parts[part]],
            send_sem=send_sem.at[send_index],
            recv_sem=arrival,
            device_id=to,
            device_id_type=MESH,
        )

    def send(index, part, to, arrival, first=False):
        copy = describe(index, part, to, arrival, len(sent), first)
        copy.start()
        sent.append(copy)

    def arrived(index, part, arrival):
        describe(index, part, pair, arrival, 0, True).wait_recv()

    def spread(zi):
        index = place(0, shifts[zi], core)
        first = zi == 0
        send(index, "all", x_up, x_sem.at[4 * zi], first)
        send(index, "all", x_down, x_sem.at[4 * zi + 1], first)
        send(index, "all", pair, pair_sem.at[4 * zi], first)

    def relay(zi):
        below, above = place(-1, shifts[zi], core), place(1, shifts[zi], core)
        arrived(below, "all", x_sem.at[4 * zi])
        send(below, "low", x_up, x_sem.at[4 * zi + 2])
        send(below, "all", pair, pair_sem.at[4 * zi + 1])
        arrived(above, "all", x_sem.at[4 * zi + 1])
        send(above, "high", x_down, x_sem.at[4 * zi + 3])
        send(above, "all", pair, pair_sem.at[4 * zi + 2])

    def finish(zi):
        far = place(2, shifts[zi], core)
        arrived(far, "low", x_sem.at[4 * zi + 2])
        arrived(far, "high", x_sem.at[4 * zi + 3])
        send(far, "all", pair, pair_sem.at[4 * zi + 3])

    own = pltpu.make_async_copy(kv_ref, out.at[me], local_sem)
    own.start()
    meet([z_up, z_down, x_up, x_down, pair])
    send(me, "all", z_up, z_sem.at[0], True)
    send(me, "all", z_down, z_sem.at[1], True)
    spread(0)
    relay(0)
    arrived(place(0, -1, core), "all", z_sem.at[0])
    send(place(0, -1, core), "low", z_up, z_sem.at[2])
    spread(1)
    arrived(place(0, 1, core), "all", z_sem.at[1])
    send(place(0, 1, core), "high", z_down, z_sem.at[3])
    spread(2)
    finish(0)
    relay(1)
    arrived(place(0, 2, core), "low", z_sem.at[2])
    arrived(place(0, 2, core), "high", z_sem.at[3])
    spread(3)
    relay(2)
    finish(1)
    finish(2)
    relay(3)
    finish(3)
    for zi in range(4):
        for xi in range(4):
            arrived(place(shifts[xi], shifts[zi], 1 - core), "all", pair_sem.at[4 * zi + xi])
    for copy in sent:
        copy.wait_send()
    own.wait()


def seq_gather(kv):
    return pl.pallas_call(
        seq_kernel,
        in_specs=[pl.BlockSpec(memory_space=SEQ_SPACE)],
        out_specs=pl.BlockSpec(memory_space=SEQ_SPACE),
        out_shape=jax.ShapeDtypeStruct((32,) + kv.shape, kv.dtype),
        scratch_shapes=[
            pltpu.SemaphoreType.DMA,
            pltpu.SemaphoreType.DMA((36,)),
            pltpu.SemaphoreType.DMA((4,)),
            pltpu.SemaphoreType.DMA((16,)),
            pltpu.SemaphoreType.DMA((16,)),
        ],
        compiler_params=pltpu.CompilerParams(collective_id=1, has_side_effects=True),
        name="seq_gather",
    )(kv)


def attend_kernel(lists, counts, q_ref, kv_hbm, out_ref, kv, sems):
    tiles = q_ref.shape[0] // TILE

    def fetch(i, j):
        return pltpu.make_async_copy(kv_hbm.at[lists[i, j]], kv.at[i, pl.ds(j * TILE, TILE)], sems.at[i])

    for i in range(tiles):
        for j in range(MAXB):
            fetch(i, j).start()

    def one_tile(i, carry):
        for j in range(MAXB):
            fetch(i, j).wait()
        rows = pl.ds(pl.multiple_of(i * TILE, TILE), TILE)

        def over(width):
            keys = kv[i, : width * TILE]
            scores = lax.dot_general(
                keys, q_ref[rows, :], (((1,), (1,)), ((), ())), preferred_element_type=jnp.float32
            )
            place = lax.broadcasted_iota(jnp.int32, scores.shape, 0)
            scores = jnp.where(place < counts[i] * TILE, scores * HD ** (-0.5), -1e30)
            top = jnp.max(scores, axis=0, keepdims=True)
            weights = jnp.exp(scores - top)
            total = jnp.sum(weights, axis=0, keepdims=True)
            summed = lax.dot_general(
                keys, weights.astype(jnp.bfloat16), (((0,), (0,)), ((), ())), preferred_element_type=jnp.float32
            )
            out_ref[:, rows] = (summed[HD:] / total).astype(jnp.bfloat16)

        for low, high in ((0, 1), (1, 2), (2, 4), (4, 8)):
            pl.when((counts[i] > low) & (counts[i] <= high))(lambda high=high: over(high))
        return carry

    lax.fori_loop(0, tiles, one_tile, 0)


def attend(lists, counts, q, kv):
    rows = q.shape[0]
    tiles = rows // TILE
    return pl.pallas_call(
        attend_kernel,
        grid_spec=pltpu.PrefetchScalarGridSpec(
            num_scalar_prefetch=2,
            grid=(1,),
            in_specs=[
                pl.BlockSpec((rows, 2 * HD), lambda i, *_: (0, 0)),
                pl.BlockSpec(memory_space=pl.ANY),
            ],
            out_specs=pl.BlockSpec((HD, rows), lambda i, *_: (0, 0)),
            scratch_shapes=[
                pltpu.VMEM((tiles, MAXB * TILE, 2 * HD), jnp.bfloat16),
                pltpu.SemaphoreType.DMA((tiles,)),
            ],
        ),
        out_shape=jax.ShapeDtypeStruct((HD, rows), jnp.bfloat16),
        name="attend",
    )(lists, counts, q, kv)


def norm_kernel(x_ref, gain_ref, out_ref):
    xf = x_ref[...].astype(jnp.float32)
    scale = lax.rsqrt(jnp.mean(xf * xf, axis=-1, keepdims=True) + 1e-05)
    out_ref[...] = (xf * scale * gain_ref[...]).astype(jnp.bfloat16)


def norm(tokens, gain):
    return pl.pallas_call(
        norm_kernel, out_shape=jax.ShapeDtypeStruct(tokens.shape, jnp.bfloat16), name="norm"
    )(tokens, gain.reshape(1, -1))


def on_device(tokens, norm_gain, w_qkv, block_lists, block_counts):
    rows, w_head = team_gather(norm(tokens, norm_gain), w_qkv)
    rows, w_head = rows.reshape(-1, rows.shape[-1]), w_head.reshape(-1, WINDOW)
    qkv = jnp.dot(rows, w_head, preferred_element_type=jnp.float32).astype(jnp.bfloat16)
    odd = lax.rem(lax.axis_index("team"), 2) == 1
    qkv = jnp.where(odd, qkv[:, HD:], qkv[:, : 3 * HD])
    q = jnp.pad(qkv[:, :HD], ((0, 0), (0, HD)))
    kv = seq_gather(qkv[:, HD:])
    return attend(block_lists, block_counts, q, kv.reshape(-1, TILE, 2 * HD)).T


def solution(mesh):
    in_specs = (P(("seq", "team"), None), P(), P("team", None), P("seq", None), P("seq"))
    out_specs = P("seq", "team")
    return jax.shard_map(
        on_device, mesh=mesh, in_specs=in_specs, out_specs=out_specs, check_vma=False
    )
```

```python
import jax
import jax.numpy as jnp
from jax import lax
from jax.experimental import pallas as pl
from jax.experimental.pallas import tpu as pltpu
from jax.sharding import PartitionSpec as P

HEADS = 16
HD = 64
TILE = 128
MAXB = 8
RING = 8
WINDOW = 256
MESH = pl.DeviceIdType.MESH
TEAM_SPACE = pltpu.VMEM
SEQ_SPACE = pl.ANY

def meet(peers):
    barrier = pltpu.get_barrier_semaphore()
    for peer in peers:
        pl.semaphore_signal(barrier, inc=1, device_id=peer, device_id_type=MESH)
    pl.semaphore_wait(barrier, len(peers))


def team_kernel(
    x_ref, w_ref, out, w_out, local_sem, send_sem, recv_sem, w_send_sem, w_recv_sem, p_send_sem, p_recv_sem
):
    me = lax.axis_index("team")
    z, y = me // RING, lax.rem(me, RING)
    other = 1 - z
    shard = lax.axis_index("seq")
    core = lax.rem(shard, 2)
    pair = {"seq": shard + 1 - 2 * core}
    depth = w_ref.shape[0]
    half = depth // 2
    mine = pl.ds(pl.multiple_of(core * half, half), half)
    theirs = pl.ds(pl.multiple_of((1 - core) * half, half), half)

    def window(head):
        return pl.ds(pl.multiple_of((3 * head) // 2 * 128, 128), WINDOW)

    def slot(plane, shift):
        return plane * RING + lax.rem(y + RING + shift, RING)

    right, left, across = {"team": slot(z, 1)}, {"team": slot(z, -1)}, {"team": slot(other, 0)}
    sent = []

    def send(src, index, to, arrival):
        copy = pltpu.make_async_remote_copy(
            src_ref=src,
            dst_ref=out.at[index],
            send_sem=send_sem.at[len(sent)],
            recv_sem=recv_sem.at[arrival],
            device_id=to,
            device_id_type=MESH,
        )
        copy.start()
        sent.append(copy)

    def arrived(index, arrival):
        pltpu.make_async_remote_copy(
            src_ref=x_ref,
            dst_ref=out.at[index],
            send_sem=send_sem.at[0],
            recv_sem=recv_sem.at[arrival],
            device_id=right,
            device_id_type=MESH,
        ).wait_recv()

    def w_copy(k):
        peer = lax.rem(me + k, HEADS)
        return pltpu.make_async_remote_copy(
            src_ref=w_ref.at[mine, window(peer)],
            dst_ref=w_out.at[me, mine],
            send_sem=w_send_sem.at[k],
            recv_sem=w_recv_sem.at[k],
            device_id={"team": peer},
            device_id_type=MESH,
        )

    def w_arrived(k):
        peer = lax.rem(me + HEADS - k, HEADS)
        pltpu.make_async_remote_copy(
            src_ref=w_ref.at[mine, window(peer)],
            dst_ref=w_out.at[peer, mine],
            send_sem=w_send_sem.at[k],
            recv_sem=w_recv_sem.at[k],
            device_id={"team": peer},
            device_id_type=MESH,
        ).wait_recv()

    def w_pass(k, rows):
        peer = lax.rem(me + HEADS - k, HEADS)
        return pltpu.make_async_remote_copy(
            src_ref=w_out.at[peer, rows],
            dst_ref=w_out.at[peer, rows],
            send_sem=p_send_sem.at[k],
            recv_sem=p_recv_sem.at[k],
            device_id=pair,
            device_id_type=MESH,
        )

    own = pltpu.make_async_copy(x_ref, out.at[me], local_sem.at[0])
    own.start()
    own_w = pltpu.make_async_copy(w_ref.at[:, window(me)], w_out.at[me], local_sem.at[1])
    own_w.start()
    meet([{"team": lax.rem(me + k, HEADS)} for k in range(1, HEADS)] + [pair])

    send(x_ref, me, right, 0)
    send(x_ref, me, left, 4)
    send(x_ref, me, across, 7)
    for k in range(1, HEADS):
        w_copy(k).start()
    arrived(slot(other, 0), 7)
    send(out.at[slot(other, 0)], slot(other, 0), right, 8)
    send(out.at[slot(other, 0)], slot(other, 0), left, 10)
    for d in (1, 2, 3):
        arrived(slot(z, -d), d - 1)
        send(out.at[slot(z, -d)], slot(z, -d), right, d)
        if d > 1:
            send(out.at[slot(z, -d)], slot(z, -d), across, 9 if d == 2 else 12)
        arrived(slot(z, d), 3 + d)
        if d < 3:
            send(out.at[slot(z, d)], slot(z, d), left, 4 + d)
        else:
            send(out.at[slot(z, 3)], slot(z, 3), across, 14)
        if d == 1:
            arrived(slot(other, 1), 10)
            send(out.at[slot(other, 1)], slot(other, 1), left, 11)
    arrived(slot(z, -4), 3)
    send(out.at[slot(z, -4)], slot(z, -4), across, 13)
    for k in range(1, HEADS):
        w_arrived(k)
        w_pass(k, mine).start()
    arrived(slot(other, -1), 8)
    arrived(slot(other, 2), 11)
    arrived(slot(other, -2), 9)
    arrived(slot(other, -3), 12)
    arrived(slot(other, 3), 14)
    arrived(slot(other, -4), 13)
    for k in range(1, HEADS):
        w_pass(k, theirs).wait_recv()
    for k in range(1, HEADS):
        w_copy(k).wait_send()
        w_pass(k, mine).wait_send()
    for copy in sent:
        copy.wait_send()
    own.wait()
    own_w.wait()


def team_gather(normed, w):
    return pl.pallas_call(
        team_kernel,
        in_specs=[pl.BlockSpec(memory_space=TEAM_SPACE)] * 2,
        out_specs=[pl.BlockSpec(memory_space=TEAM_SPACE)] * 2,
        out_shape=[
            jax.ShapeDtypeStruct((HEADS,) + normed.shape, normed.dtype),
            jax.ShapeDtypeStruct((HEADS, w.shape[0], WINDOW), w.dtype),
        ],
        scratch_shapes=[
            pltpu.SemaphoreType.DMA((2,)),
            pltpu.SemaphoreType.DMA((15,)),
            pltpu.SemaphoreType.DMA((15,)),
            pltpu.SemaphoreType.DMA((HEADS,)),
            pltpu.SemaphoreType.DMA((HEADS,)),
            pltpu.SemaphoreType.DMA((HEADS,)),
            pltpu.SemaphoreType.DMA((HEADS,)),
        ],
        compiler_params=pltpu.CompilerParams(collective_id=0, has_side_effects=True),
        name="team_gather",
    )(normed, w)


def seq_kernel(kv_ref, out, local_sem, send_sem, z_sem, x_sem, pair_sem):
    me = lax.axis_index("seq")
    x, z, core = me // 8, lax.rem(me // 2, 4), lax.rem(me, 2)
    half = kv_ref.shape[0] // 2
    shifts = (0, -1, 1, 2)

    def place(xs, zs, c):
        return lax.rem(x + 4 + xs, 4) * 8 + lax.rem(z + 4 + zs, 4) * 2 + c

    z_up, z_down = {"seq": place(0, 1, core)}, {"seq": place(0, -1, core)}
    x_up, x_down = {"seq": place(1, 0, core)}, {"seq": place(-1, 0, core)}
    pair = {"seq": place(0, 0, 1 - core)}
    parts = {"all": pl.ds(0, 2 * half), "low": pl.ds(0, half), "high": pl.ds(half, half)}
    sent = []

    def describe(index, part, to, arrival, send_index, first):
        src = kv_ref if first else out.at[index]
        return pltpu.make_async_remote_copy(
            src_ref=src.at[parts[part]],
            dst_ref=out.at[index, parts[part]],
            send_sem=send_sem.at[send_index],
            recv_sem=arrival,
            device_id=to,
            device_id_type=MESH,
        )

    def send(index, part, to, arrival, first=False):
        copy = describe(index, part, to, arrival, len(sent), first)
        copy.start()
        sent.append(copy)

    def arrived(index, part, arrival):
        describe(index, part, pair, arrival, 0, True).wait_recv()

    def spread(zi, part):
        index = place(0, shifts[zi], core)
        offset = 0 if part == "low" else 1
        send(index, part, x_up, x_sem.at[6 * zi + offset], zi == 0)
        send(index, part, x_down, x_sem.at[6 * zi + 2 + offset], zi == 0)

    def share(zi, xi):
        send(place(shifts[xi], shifts[zi], core), "all", pair, pair_sem.at[4 * zi + xi], zi + xi == 0)

    def relay(zi):
        below, above = place(-1, shifts[zi], core), place(1, shifts[zi], core)
        arrived(below, "low", x_sem.at[6 * zi])
        send(below, "low", x_up, x_sem.at[6 * zi + 4])
        arrived(above, "high", x_sem.at[6 * zi + 3])
        send(above, "high", x_down, x_sem.at[6 * zi + 5])

    def settle(zi):
        arrived(place(-1, shifts[zi], core), "high", x_sem.at[6 * zi + 1])
        share(zi, 1)
        arrived(place(1, shifts[zi], core), "low", x_sem.at[6 * zi + 2])
        share(zi, 2)

    def finish(zi):
        far = place(2, shifts[zi], core)
        arrived(far, "low", x_sem.at[6 * zi + 4])
        arrived(far, "high", x_sem.at[6 * zi + 5])
        share(zi, 3)

    own = pltpu.make_async_copy(kv_ref, out.at[me], local_sem)
    own.start()
    meet([z_up, z_down, x_up, x_down, pair])
    send(me, "low", z_up, z_sem.at[0], True)
    send(me, "high", z_down, z_sem.at[3], True)
    spread(0, "low")
    spread(0, "high")
    send(me, "high", z_up, z_sem.at[1], True)
    send(me, "low", z_down, z_sem.at[2], True)
    share(0, 0)
    relay(0)
    arrived(place(0, -1, core), "low", z_sem.at[0])
    send(place(0, -1, core), "low", z_up, z_sem.at[4])
    spread(1, "low")
    arrived(place(0, 1, core), "high", z_sem.at[3])
    send(place(0, 1, core), "high", z_down, z_sem.at[5])
    spread(2, "high")
    settle(0)
    arrived(place(0, -1, core), "high", z_sem.at[1])
    spread(1, "high")
    share(1, 0)
    arrived(place(0, 1, core), "low", z_sem.at[2])
    spread(2, "low")
    share(2, 0)
    finish(0)
    relay(1)
    arrived(place(0, 2, core), "low", z_sem.at[4])
    spread(3, "low")
    arrived(place(0, 2, core), "high", z_sem.at[5])
    spread(3, "high")
    share(3, 0)
    relay(2)
    settle(1)
    settle(2)
    relay(3)
    finish(1)
    finish(2)
    settle(3)
    finish(3)
    for zi in range(4):
        for xi in range(4):
            arrived(place(shifts[xi], shifts[zi], 1 - core), "all", pair_sem.at[4 * zi + xi])
    for copy in sent:
        copy.wait_send()
    own.wait()


def seq_gather(kv):
    return pl.pallas_call(
        seq_kernel,
        in_specs=[pl.BlockSpec(memory_space=SEQ_SPACE)],
        out_specs=pl.BlockSpec(memory_space=SEQ_SPACE),
        out_shape=jax.ShapeDtypeStruct((32,) + kv.shape, kv.dtype),
        scratch_shapes=[
            pltpu.SemaphoreType.DMA,
            pltpu.SemaphoreType.DMA((46,)),
            pltpu.SemaphoreType.DMA((6,)),
            pltpu.SemaphoreType.DMA((24,)),
            pltpu.SemaphoreType.DMA((16,)),
        ],
        compiler_params=pltpu.CompilerParams(collective_id=1, has_side_effects=True),
        name="seq_gather",
    )(kv)


def attend_kernel(lists, counts, q_ref, kv_hbm, out_ref, kv, sems):
    tiles = q_ref.shape[0] // TILE

    def fetch(i, j):
        return pltpu.make_async_copy(kv_hbm.at[lists[i, j]], kv.at[i, pl.ds(j * TILE, TILE)], sems.at[i])

    for i in range(tiles):
        for j in range(MAXB):
            fetch(i, j).start()

    def one_tile(i, carry):
        for j in range(MAXB):
            fetch(i, j).wait()
        rows = pl.ds(pl.multiple_of(i * TILE, TILE), TILE)

        def over(width):
            keys = kv[i, : width * TILE]
            scores = lax.dot_general(
                keys, q_ref[rows, :], (((1,), (1,)), ((), ())), preferred_element_type=jnp.float32
            )
            place = lax.broadcasted_iota(jnp.int32, scores.shape, 0)
            scores = jnp.where(place < counts[i] * TILE, scores * HD ** (-0.5), -1e30)
            top = jnp.max(scores, axis=0, keepdims=True)
            weights = jnp.exp(scores - top)
            total = jnp.sum(weights, axis=0, keepdims=True)
            summed = lax.dot_general(
                keys, weights.astype(jnp.bfloat16), (((0,), (0,)), ((), ())), preferred_element_type=jnp.float32
            )
            out_ref[:, rows] = (summed[HD:] / total).astype(jnp.bfloat16)

        for low, high in ((0, 1), (1, 2), (2, 4), (4, 8)):
            pl.when((counts[i] > low) & (counts[i] <= high))(lambda high=high: over(high))
        return carry

    lax.fori_loop(0, tiles, one_tile, 0)


def attend(lists, counts, q, kv):
    rows = q.shape[0]
    tiles = rows // TILE
    return pl.pallas_call(
        attend_kernel,
        grid_spec=pltpu.PrefetchScalarGridSpec(
            num_scalar_prefetch=2,
            grid=(1,),
            in_specs=[
                pl.BlockSpec((rows, 2 * HD), lambda i, *_: (0, 0)),
                pl.BlockSpec(memory_space=pl.ANY),
            ],
            out_specs=pl.BlockSpec((HD, rows), lambda i, *_: (0, 0)),
            scratch_shapes=[
                pltpu.VMEM((tiles, MAXB * TILE, 2 * HD), jnp.bfloat16),
                pltpu.SemaphoreType.DMA((tiles,)),
            ],
        ),
        out_shape=jax.ShapeDtypeStruct((HD, rows), jnp.bfloat16),
        name="attend",
    )(lists, counts, q, kv)


def norm_kernel(x_ref, gain_ref, out_ref):
    xf = x_ref[...].astype(jnp.float32)
    scale = lax.rsqrt(jnp.mean(xf * xf, axis=-1, keepdims=True) + 1e-05)
    out_ref[...] = (xf * scale * gain_ref[...]).astype(jnp.bfloat16)


def norm(tokens, gain):
    return pl.pallas_call(
        norm_kernel, out_shape=jax.ShapeDtypeStruct(tokens.shape, jnp.bfloat16), name="norm"
    )(tokens, gain.reshape(1, -1))


def project_kernel(odd, x_ref, w_ref, q_ref, kv_ref):
    qkv = jnp.dot(x_ref[...], w_ref[...], preferred_element_type=jnp.float32)
    qkv = jnp.where(odd[0] == 1, pltpu.roll(qkv, WINDOW - HD, 1), qkv)
    query = qkv[:, : 2 * HD]
    lane = lax.broadcasted_iota(jnp.int32, query.shape, 1)
    q_ref[...] = jnp.where(lane < HD, query, 0.0).astype(jnp.bfloat16)
    kv_ref[...] = pltpu.roll(qkv, WINDOW - HD, 1)[:, : 2 * HD].astype(jnp.bfloat16)


def project(rows, w, odd, block=256):
    count, depth = rows.shape
    return pl.pallas_call(
        project_kernel,
        grid_spec=pltpu.PrefetchScalarGridSpec(
            num_scalar_prefetch=1,
            grid=(count // block,),
            in_specs=[
                pl.BlockSpec((block, depth), lambda i, *_: (i, 0)),
                pl.BlockSpec((depth, WINDOW), lambda i, *_: (0, 0)),
            ],
            out_specs=[pl.BlockSpec((block, 2 * HD), lambda i, *_: (i, 0))] * 2,
        ),
        out_shape=[jax.ShapeDtypeStruct((count, 2 * HD), jnp.bfloat16)] * 2,
        name="project",
    )(odd, rows, w)


def on_device(tokens, norm_gain, w_qkv, block_lists, block_counts):
    rows, w_head = team_gather(norm(tokens, norm_gain), w_qkv)
    odd = lax.rem(lax.axis_index("team"), 2).astype(jnp.int32).reshape(1)
    q, kv = project(rows.reshape(-1, rows.shape[-1]), w_head.reshape(-1, WINDOW), odd)
    kv = seq_gather(kv)
    return attend(block_lists, block_counts, q, kv.reshape(-1, TILE, 2 * HD)).T


def solution(mesh):
    in_specs = (P(("seq", "team"), None), P(), P("team", None), P("seq", None), P("seq"))
    out_specs = P("seq", "team")
    return jax.shard_map(
        on_device, mesh=mesh, in_specs=in_specs, out_specs=out_specs, check_vma=False
    )
```

```python
import jax
import jax.numpy as jnp
from jax import lax
from jax.experimental import pallas as pl
from jax.experimental.pallas import tpu as pltpu
from jax.sharding import PartitionSpec as P

HEADS = 16
HD = 64
TILE = 128
MAXB = 8
RING = 8
WINDOW = 256
MESH = pl.DeviceIdType.MESH
TEAM_SPACE = pl.ANY
SEQ_SPACE = pl.ANY

def meet(peers):
    barrier = pltpu.get_barrier_semaphore()
    for peer in peers:
        pl.semaphore_signal(barrier, inc=1, device_id=peer, device_id_type=MESH)
    pl.semaphore_wait(barrier, len(peers))


def team_kernel(
    x_ref, w_ref, out, w_out, local_sem, send_sem, recv_sem, w_send_sem, w_recv_sem, p_send_sem, p_recv_sem
):
    me = lax.axis_index("team")
    z, y = me // RING, lax.rem(me, RING)
    other = 1 - z
    shard = lax.axis_index("seq")
    core = lax.rem(shard, 2)
    pair = {"seq": shard + 1 - 2 * core}
    depth = w_ref.shape[0]
    half = depth // 2
    mine = pl.ds(pl.multiple_of(core * half, half), half)
    theirs = pl.ds(pl.multiple_of((1 - core) * half, half), half)

    def window(head):
        return pl.ds(pl.multiple_of((3 * head) // 2 * 128, 128), WINDOW)

    def slot(plane, shift):
        return plane * RING + lax.rem(y + RING + shift, RING)

    right, left, across = {"team": slot(z, 1)}, {"team": slot(z, -1)}, {"team": slot(other, 0)}
    sent = []

    def send(src, index, to, arrival):
        copy = pltpu.make_async_remote_copy(
            src_ref=src,
            dst_ref=out.at[index],
            send_sem=send_sem.at[len(sent)],
            recv_sem=recv_sem.at[arrival],
            device_id=to,
            device_id_type=MESH,
        )
        copy.start()
        sent.append(copy)

    def arrived(index, arrival):
        pltpu.make_async_remote_copy(
            src_ref=x_ref,
            dst_ref=out.at[index],
            send_sem=send_sem.at[0],
            recv_sem=recv_sem.at[arrival],
            device_id=right,
            device_id_type=MESH,
        ).wait_recv()

    def w_copy(k):
        peer = lax.rem(me + k, HEADS)
        return pltpu.make_async_remote_copy(
            src_ref=w_ref.at[mine, window(peer)],
            dst_ref=w_out.at[me, mine],
            send_sem=w_send_sem.at[k],
            recv_sem=w_recv_sem.at[k],
            device_id={"team": peer},
            device_id_type=MESH,
        )

    def w_arrived(k):
        peer = lax.rem(me + HEADS - k, HEADS)
        pltpu.make_async_remote_copy(
            src_ref=w_ref.at[mine, window(peer)],
            dst_ref=w_out.at[peer, mine],
            send_sem=w_send_sem.at[k],
            recv_sem=w_recv_sem.at[k],
            device_id={"team": peer},
            device_id_type=MESH,
        ).wait_recv()

    def w_pass(k, rows):
        peer = lax.rem(me + HEADS - k, HEADS)
        return pltpu.make_async_remote_copy(
            src_ref=w_out.at[peer, rows],
            dst_ref=w_out.at[peer, rows],
            send_sem=p_send_sem.at[k],
            recv_sem=p_recv_sem.at[k],
            device_id=pair,
            device_id_type=MESH,
        )

    own = pltpu.make_async_copy(x_ref, out.at[me], local_sem.at[0])
    own.start()
    own_w = pltpu.make_async_copy(w_ref.at[:, window(me)], w_out.at[me], local_sem.at[1])
    own_w.start()
    meet([{"team": lax.rem(me + k, HEADS)} for k in range(1, HEADS)] + [pair])

    send(x_ref, me, right, 0)
    send(x_ref, me, left, 4)
    send(x_ref, me, across, 7)
    for k in range(1, HEADS):
        w_copy(k).start()
    arrived(slot(other, 0), 7)
    send(out.at[slot(other, 0)], slot(other, 0), right, 8)
    send(out.at[slot(other, 0)], slot(other, 0), left, 10)
    for d in (1, 2, 3):
        arrived(slot(z, -d), d - 1)
        send(out.at[slot(z, -d)], slot(z, -d), right, d)
        if d > 1:
            send(out.at[slot(z, -d)], slot(z, -d), across, 9 if d == 2 else 12)
        arrived(slot(z, d), 3 + d)
        if d < 3:
            send(out.at[slot(z, d)], slot(z, d), left, 4 + d)
        else:
            send(out.at[slot(z, 3)], slot(z, 3), across, 14)
        if d == 1:
            arrived(slot(other, 1), 10)
            send(out.at[slot(other, 1)], slot(other, 1), left, 11)
    arrived(slot(z, -4), 3)
    send(out.at[slot(z, -4)], slot(z, -4), across, 13)
    for k in range(1, HEADS):
        w_arrived(k)
        w_pass(k, mine).start()
    arrived(slot(other, -1), 8)
    arrived(slot(other, 2), 11)
    arrived(slot(other, -2), 9)
    arrived(slot(other, -3), 12)
    arrived(slot(other, 3), 14)
    arrived(slot(other, -4), 13)
    for k in range(1, HEADS):
        w_pass(k, theirs).wait_recv()
    for k in range(1, HEADS):
        w_copy(k).wait_send()
        w_pass(k, mine).wait_send()
    for copy in sent:
        copy.wait_send()
    own.wait()
    own_w.wait()


def team_gather(normed, w):
    return pl.pallas_call(
        team_kernel,
        in_specs=[pl.BlockSpec(memory_space=TEAM_SPACE)] * 2,
        out_specs=[pl.BlockSpec(memory_space=TEAM_SPACE)] * 2,
        out_shape=[
            jax.ShapeDtypeStruct((HEADS,) + normed.shape, normed.dtype),
            jax.ShapeDtypeStruct((HEADS, w.shape[0], WINDOW), w.dtype),
        ],
        scratch_shapes=[
            pltpu.SemaphoreType.DMA((2,)),
            pltpu.SemaphoreType.DMA((15,)),
            pltpu.SemaphoreType.DMA((15,)),
            pltpu.SemaphoreType.DMA((HEADS,)),
            pltpu.SemaphoreType.DMA((HEADS,)),
            pltpu.SemaphoreType.DMA((HEADS,)),
            pltpu.SemaphoreType.DMA((HEADS,)),
        ],
        compiler_params=pltpu.CompilerParams(collective_id=0, has_side_effects=True),
        name="team_gather",
    )(normed, w)


def seq_kernel(kv_ref, out, local_sem, send_sem, z_sem, x_sem, pair_sem):
    me = lax.axis_index("seq")
    x, z, core = me // 8, lax.rem(me // 2, 4), lax.rem(me, 2)
    half = kv_ref.shape[0] // 2
    shifts = (0, -1, 1, 2)

    def place(xs, zs, c):
        return lax.rem(x + 4 + xs, 4) * 8 + lax.rem(z + 4 + zs, 4) * 2 + c

    z_up, z_down = {"seq": place(0, 1, core)}, {"seq": place(0, -1, core)}
    x_up, x_down = {"seq": place(1, 0, core)}, {"seq": place(-1, 0, core)}
    pair = {"seq": place(0, 0, 1 - core)}
    parts = {"all": pl.ds(0, 2 * half), "low": pl.ds(0, half), "high": pl.ds(half, half)}
    sent = []

    def describe(index, part, to, arrival, send_index, first):
        src = kv_ref if first else out.at[index]
        return pltpu.make_async_remote_copy(
            src_ref=src.at[parts[part]],
            dst_ref=out.at[index, parts[part]],
            send_sem=send_sem.at[send_index],
            recv_sem=arrival,
            device_id=to,
            device_id_type=MESH,
        )

    def send(index, part, to, arrival, first=False):
        copy = describe(index, part, to, arrival, len(sent), first)
        copy.start()
        sent.append(copy)

    def arrived(index, part, arrival):
        describe(index, part, pair, arrival, 0, True).wait_recv()

    def spread(zi, part):
        index = place(0, shifts[zi], core)
        offset = 0 if part == "low" else 1
        send(index, part, x_up, x_sem.at[6 * zi + offset], zi == 0)
        send(index, part, x_down, x_sem.at[6 * zi + 2 + offset], zi == 0)

    def share(zi, xi):
        send(place(shifts[xi], shifts[zi], core), "all", pair, pair_sem.at[4 * zi + xi], zi + xi == 0)

    def relay(zi):
        below, above = place(-1, shifts[zi], core), place(1, shifts[zi], core)
        arrived(below, "low", x_sem.at[6 * zi])
        send(below, "low", x_up, x_sem.at[6 * zi + 4])
        arrived(above, "high", x_sem.at[6 * zi + 3])
        send(above, "high", x_down, x_sem.at[6 * zi + 5])

    def settle(zi):
        arrived(place(-1, shifts[zi], core), "high", x_sem.at[6 * zi + 1])
        share(zi, 1)
        arrived(place(1, shifts[zi], core), "low", x_sem.at[6 * zi + 2])
        share(zi, 2)

    def finish(zi):
        far = place(2, shifts[zi], core)
        arrived(far, "low", x_sem.at[6 * zi + 4])
        arrived(far, "high", x_sem.at[6 * zi + 5])
        share(zi, 3)

    own = pltpu.make_async_copy(kv_ref, out.at[me], local_sem)
    own.start()
    meet([z_up, z_down, x_up, x_down, pair])
    send(me, "low", z_up, z_sem.at[0], True)
    send(me, "high", z_down, z_sem.at[3], True)
    spread(0, "low")
    spread(0, "high")
    send(me, "high", z_up, z_sem.at[1], True)
    send(me, "low", z_down, z_sem.at[2], True)
    share(0, 0)
    relay(0)
    arrived(place(0, -1, core), "low", z_sem.at[0])
    send(place(0, -1, core), "low", z_up, z_sem.at[4])
    spread(1, "low")
    arrived(place(0, 1, core), "high", z_sem.at[3])
    send(place(0, 1, core), "high", z_down, z_sem.at[5])
    spread(2, "high")
    settle(0)
    arrived(place(0, -1, core), "high", z_sem.at[1])
    spread(1, "high")
    share(1, 0)
    arrived(place(0, 1, core), "low", z_sem.at[2])
    spread(2, "low")
    share(2, 0)
    finish(0)
    relay(1)
    arrived(place(0, 2, core), "low", z_sem.at[4])
    spread(3, "low")
    arrived(place(0, 2, core), "high", z_sem.at[5])
    spread(3, "high")
    share(3, 0)
    relay(2)
    settle(1)
    settle(2)
    relay(3)
    finish(1)
    finish(2)
    settle(3)
    finish(3)
    for zi in range(4):
        for xi in range(4):
            arrived(place(shifts[xi], shifts[zi], 1 - core), "all", pair_sem.at[4 * zi + xi])
    for copy in sent:
        copy.wait_send()
    own.wait()


def seq_gather(kv):
    return pl.pallas_call(
        seq_kernel,
        in_specs=[pl.BlockSpec(memory_space=SEQ_SPACE)],
        out_specs=pl.BlockSpec(memory_space=SEQ_SPACE),
        out_shape=jax.ShapeDtypeStruct((32,) + kv.shape, kv.dtype),
        scratch_shapes=[
            pltpu.SemaphoreType.DMA,
            pltpu.SemaphoreType.DMA((46,)),
            pltpu.SemaphoreType.DMA((6,)),
            pltpu.SemaphoreType.DMA((24,)),
            pltpu.SemaphoreType.DMA((16,)),
        ],
        compiler_params=pltpu.CompilerParams(collective_id=1, has_side_effects=True),
        name="seq_gather",
    )(kv)


def attend_kernel(lists, counts, q_ref, kv_hbm, out_ref, kv, sems):
    tiles = q_ref.shape[0] // TILE

    def fetch(i, j):
        return pltpu.make_async_copy(kv_hbm.at[lists[i, j]], kv.at[i, pl.ds(j * TILE, TILE)], sems.at[i])

    for i in range(tiles):
        for j in range(MAXB):
            fetch(i, j).start()

    def one_tile(i, carry):
        for j in range(MAXB):
            fetch(i, j).wait()
        rows = pl.ds(pl.multiple_of(i * TILE, TILE), TILE)

        def over(width):
            keys = kv[i, : width * TILE]
            scores = lax.dot_general(
                keys, q_ref[rows, :], (((1,), (1,)), ((), ())), preferred_element_type=jnp.float32
            )
            place = lax.broadcasted_iota(jnp.int32, scores.shape, 0)
            scores = jnp.where(place < counts[i] * TILE, scores * HD ** (-0.5), -1e30)
            top = jnp.max(scores, axis=0, keepdims=True)
            weights = jnp.exp(scores - top)
            total = jnp.sum(weights, axis=0, keepdims=True)
            summed = lax.dot_general(
                keys, weights.astype(jnp.bfloat16), (((0,), (0,)), ((), ())), preferred_element_type=jnp.float32
            )
            out_ref[:, rows] = (summed[HD:] / total).astype(jnp.bfloat16)

        for low, high in ((0, 1), (1, 2), (2, 4), (4, 8)):
            pl.when((counts[i] > low) & (counts[i] <= high))(lambda high=high: over(high))
        return carry

    lax.fori_loop(0, tiles, one_tile, 0)


def attend(lists, counts, q, kv):
    rows = q.shape[0]
    tiles = rows // TILE
    return pl.pallas_call(
        attend_kernel,
        grid_spec=pltpu.PrefetchScalarGridSpec(
            num_scalar_prefetch=2,
            grid=(1,),
            in_specs=[
                pl.BlockSpec((rows, 2 * HD), lambda i, *_: (0, 0)),
                pl.BlockSpec(memory_space=pl.ANY),
            ],
            out_specs=pl.BlockSpec((HD, rows), lambda i, *_: (0, 0)),
            scratch_shapes=[
                pltpu.VMEM((tiles, MAXB * TILE, 2 * HD), jnp.bfloat16),
                pltpu.SemaphoreType.DMA((tiles,)),
            ],
        ),
        out_shape=jax.ShapeDtypeStruct((HD, rows), jnp.bfloat16),
        name="attend",
    )(lists, counts, q, kv)


def norm_kernel(x_ref, gain_ref, out_ref):
    xf = x_ref[...].astype(jnp.float32)
    scale = lax.rsqrt(jnp.mean(xf * xf, axis=-1, keepdims=True) + 1e-05)
    out_ref[...] = (xf * scale * gain_ref[...]).astype(jnp.bfloat16)


def norm(tokens, gain):
    return pl.pallas_call(
        norm_kernel, out_shape=jax.ShapeDtypeStruct(tokens.shape, jnp.bfloat16), name="norm"
    )(tokens, gain.reshape(1, -1))


def on_device(tokens, norm_gain, w_qkv, block_lists, block_counts):
    rows, w_head = team_gather(norm(tokens, norm_gain), w_qkv)
    rows, w_head = rows.reshape(-1, rows.shape[-1]), w_head.reshape(-1, WINDOW)
    qkv = jnp.dot(rows, w_head, preferred_element_type=jnp.float32).astype(jnp.bfloat16)
    odd = lax.rem(lax.axis_index("team"), 2) == 1
    qkv = jnp.where(odd, qkv[:, HD:], qkv[:, : 3 * HD])
    q = jnp.pad(qkv[:, :HD], ((0, 0), (0, HD)))
    kv = seq_gather(qkv[:, HD:])
    return attend(block_lists, block_counts, q, kv.reshape(-1, TILE, 2 * HD)).T


def solution(mesh):
    in_specs = (P(("seq", "team"), None), P(), P("team", None), P("seq", None), P("seq"))
    out_specs = P("seq", "team")
    return jax.shard_map(
        on_device, mesh=mesh, in_specs=in_specs, out_specs=out_specs, check_vma=False
    )
```

```python
import jax
import jax.numpy as jnp
from jax import lax
from jax.experimental import pallas as pl
from jax.experimental.pallas import tpu as pltpu
from jax.sharding import PartitionSpec as P

HEADS = 16
HD = 64
TILE = 128
MAXB = 8
RING = 8
WINDOW = 256
MESH = pl.DeviceIdType.MESH
TEAM_SPACE = pl.ANY
SEQ_SPACE = pl.ANY

def meet(peers):
    barrier = pltpu.get_barrier_semaphore()
    for peer in peers:
        pl.semaphore_signal(barrier, inc=1, device_id=peer, device_id_type=MESH)
    pl.semaphore_wait(barrier, len(peers))


def team_kernel(
    x_ref, w_ref, out, w_out, local_sem, send_sem, recv_sem, w_send_sem, w_recv_sem, p_send_sem, p_recv_sem
):
    me = lax.axis_index("team")
    z, y = me // RING, lax.rem(me, RING)
    other = 1 - z
    shard = lax.axis_index("seq")
    core = lax.rem(shard, 2)
    pair = {"seq": shard + 1 - 2 * core}
    depth = w_ref.shape[0]
    half = depth // 2
    mine = pl.ds(pl.multiple_of(core * half, half), half)
    theirs = pl.ds(pl.multiple_of((1 - core) * half, half), half)

    def window(head):
        return pl.ds(pl.multiple_of((3 * head) // 2 * 128, 128), WINDOW)

    def slot(plane, shift):
        return plane * RING + lax.rem(y + RING + shift, RING)

    right, left, across = {"team": slot(z, 1)}, {"team": slot(z, -1)}, {"team": slot(other, 0)}
    sent = []

    def send(src, index, to, arrival):
        copy = pltpu.make_async_remote_copy(
            src_ref=src,
            dst_ref=out.at[index],
            send_sem=send_sem.at[len(sent)],
            recv_sem=recv_sem.at[arrival],
            device_id=to,
            device_id_type=MESH,
        )
        copy.start()
        sent.append(copy)

    def arrived(index, arrival):
        pltpu.make_async_remote_copy(
            src_ref=x_ref,
            dst_ref=out.at[index],
            send_sem=send_sem.at[0],
            recv_sem=recv_sem.at[arrival],
            device_id=right,
            device_id_type=MESH,
        ).wait_recv()

    def w_copy(k):
        peer = lax.rem(me + k, HEADS)
        return pltpu.make_async_remote_copy(
            src_ref=w_ref.at[mine, window(peer)],
            dst_ref=w_out.at[me, mine],
            send_sem=w_send_sem.at[k],
            recv_sem=w_recv_sem.at[k],
            device_id={"team": peer},
            device_id_type=MESH,
        )

    def w_arrived(k):
        peer = lax.rem(me + HEADS - k, HEADS)
        pltpu.make_async_remote_copy(
            src_ref=w_ref.at[mine, window(peer)],
            dst_ref=w_out.at[peer, mine],
            send_sem=w_send_sem.at[k],
            recv_sem=w_recv_sem.at[k],
            device_id={"team": peer},
            device_id_type=MESH,
        ).wait_recv()

    def w_pass(k, rows):
        peer = lax.rem(me + HEADS - k, HEADS)
        return pltpu.make_async_remote_copy(
            src_ref=w_out.at[peer, rows],
            dst_ref=w_out.at[peer, rows],
            send_sem=p_send_sem.at[k],
            recv_sem=p_recv_sem.at[k],
            device_id=pair,
            device_id_type=MESH,
        )

    own = pltpu.make_async_copy(x_ref, out.at[me], local_sem.at[0])
    own.start()
    own_w = pltpu.make_async_copy(w_ref.at[:, window(me)], w_out.at[me], local_sem.at[1])
    own_w.start()
    meet([{"team": lax.rem(me + k, HEADS)} for k in range(1, HEADS)] + [pair])

    send(x_ref, me, right, 0)
    send(x_ref, me, left, 4)
    send(x_ref, me, across, 7)
    arrived(slot(other, 0), 7)
    send(out.at[slot(other, 0)], slot(other, 0), right, 8)
    send(out.at[slot(other, 0)], slot(other, 0), left, 10)
    for d in (1, 2, 3):
        arrived(slot(z, -d), d - 1)
        send(out.at[slot(z, -d)], slot(z, -d), right, d)
        if d > 1:
            send(out.at[slot(z, -d)], slot(z, -d), across, 9 if d == 2 else 12)
        arrived(slot(z, d), 3 + d)
        if d < 3:
            send(out.at[slot(z, d)], slot(z, d), left, 4 + d)
        else:
            send(out.at[slot(z, 3)], slot(z, 3), across, 14)
        if d == 1:
            arrived(slot(other, 1), 10)
            send(out.at[slot(other, 1)], slot(other, 1), left, 11)
        for k in range(5 * d - 4, 5 * d + 1):
            w_copy(k).start()
    arrived(slot(z, -4), 3)
    send(out.at[slot(z, -4)], slot(z, -4), across, 13)
    for k in range(1, HEADS):
        w_arrived(k)
        w_pass(k, mine).start()
    arrived(slot(other, -1), 8)
    arrived(slot(other, 2), 11)
    arrived(slot(other, -2), 9)
    arrived(slot(other, -3), 12)
    arrived(slot(other, 3), 14)
    arrived(slot(other, -4), 13)
    for k in range(1, HEADS):
        w_pass(k, theirs).wait_recv()
    for k in range(1, HEADS):
        w_copy(k).wait_send()
        w_pass(k, mine).wait_send()
    for copy in sent:
        copy.wait_send()
    own.wait()
    own_w.wait()


def team_gather(normed, w):
    return pl.pallas_call(
        team_kernel,
        in_specs=[pl.BlockSpec(memory_space=TEAM_SPACE)] * 2,
        out_specs=[pl.BlockSpec(memory_space=TEAM_SPACE)] * 2,
        out_shape=[
            jax.ShapeDtypeStruct((HEADS,) + normed.shape, normed.dtype),
            jax.ShapeDtypeStruct((HEADS, w.shape[0], WINDOW), w.dtype),
        ],
        scratch_shapes=[
            pltpu.SemaphoreType.DMA((2,)),
            pltpu.SemaphoreType.DMA((15,)),
            pltpu.SemaphoreType.DMA((15,)),
            pltpu.SemaphoreType.DMA((HEADS,)),
            pltpu.SemaphoreType.DMA((HEADS,)),
            pltpu.SemaphoreType.DMA((HEADS,)),
            pltpu.SemaphoreType.DMA((HEADS,)),
        ],
        compiler_params=pltpu.CompilerParams(collective_id=0, has_side_effects=True),
        name="team_gather",
    )(normed, w)


def seq_kernel(kv_ref, out, local_sem, send_sem, z_sem, x_sem, pair_sem):
    me = lax.axis_index("seq")
    x, z, core = me // 8, lax.rem(me // 2, 4), lax.rem(me, 2)
    half = kv_ref.shape[0] // 2
    shifts = (0, -1, 1, 2)

    def place(xs, zs, c):
        return lax.rem(x + 4 + xs, 4) * 8 + lax.rem(z + 4 + zs, 4) * 2 + c

    z_up, z_down = {"seq": place(0, 1, core)}, {"seq": place(0, -1, core)}
    x_up, x_down = {"seq": place(1, 0, core)}, {"seq": place(-1, 0, core)}
    pair = {"seq": place(0, 0, 1 - core)}
    parts = {"all": pl.ds(0, 2 * half), "low": pl.ds(0, half), "high": pl.ds(half, half)}
    sent = []

    def describe(index, part, to, arrival, send_index, first):
        src = kv_ref if first else out.at[index]
        return pltpu.make_async_remote_copy(
            src_ref=src.at[parts[part]],
            dst_ref=out.at[index, parts[part]],
            send_sem=send_sem.at[send_index],
            recv_sem=arrival,
            device_id=to,
            device_id_type=MESH,
        )

    def send(index, part, to, arrival, first=False):
        copy = describe(index, part, to, arrival, len(sent), first)
        copy.start()
        sent.append(copy)

    def arrived(index, part, arrival):
        describe(index, part, pair, arrival, 0, True).wait_recv()

    def spread(zi, part):
        index = place(0, shifts[zi], core)
        offset = 0 if part == "low" else 1
        send(index, part, x_up, x_sem.at[6 * zi + offset], zi == 0)
        send(index, part, x_down, x_sem.at[6 * zi + 2 + offset], zi == 0)

    def share(zi, xi):
        send(place(shifts[xi], shifts[zi], core), "all", pair, pair_sem.at[4 * zi + xi], zi + xi == 0)

    def relay(zi):
        below, above = place(-1, shifts[zi], core), place(1, shifts[zi], core)
        arrived(below, "low", x_sem.at[6 * zi])
        send(below, "low", x_up, x_sem.at[6 * zi + 4])
        arrived(above, "high", x_sem.at[6 * zi + 3])
        send(above, "high", x_down, x_sem.at[6 * zi + 5])

    def settle(zi):
        arrived(place(-1, shifts[zi], core), "high", x_sem.at[6 * zi + 1])
        share(zi, 1)
        arrived(place(1, shifts[zi], core), "low", x_sem.at[6 * zi + 2])
        share(zi, 2)

    def finish(zi):
        far = place(2, shifts[zi], core)
        arrived(far, "low", x_sem.at[6 * zi + 4])
        arrived(far, "high", x_sem.at[6 * zi + 5])
        share(zi, 3)

    own = pltpu.make_async_copy(kv_ref, out.at[me], local_sem)
    own.start()
    meet([z_up, z_down, x_up, x_down, pair])
    send(me, "low", z_up, z_sem.at[0], True)
    send(me, "high", z_down, z_sem.at[3], True)
    spread(0, "low")
    spread(0, "high")
    send(me, "high", z_up, z_sem.at[1], True)
    send(me, "low", z_down, z_sem.at[2], True)
    share(0, 0)
    relay(0)
    arrived(place(0, -1, core), "low", z_sem.at[0])
    send(place(0, -1, core), "low", z_up, z_sem.at[4])
    spread(1, "low")
    arrived(place(0, 1, core), "high", z_sem.at[3])
    send(place(0, 1, core), "high", z_down, z_sem.at[5])
    spread(2, "high")
    settle(0)
    arrived(place(0, -1, core), "high", z_sem.at[1])
    spread(1, "high")
    share(1, 0)
    arrived(place(0, 1, core), "low", z_sem.at[2])
    spread(2, "low")
    share(2, 0)
    finish(0)
    relay(1)
    arrived(place(0, 2, core), "low", z_sem.at[4])
    spread(3, "low")
    arrived(place(0, 2, core), "high", z_sem.at[5])
    spread(3, "high")
    share(3, 0)
    relay(2)
    settle(1)
    settle(2)
    relay(3)
    finish(1)
    finish(2)
    settle(3)
    finish(3)
    for zi in range(4):
        for xi in range(4):
            arrived(place(shifts[xi], shifts[zi], 1 - core), "all", pair_sem.at[4 * zi + xi])
    for copy in sent:
        copy.wait_send()
    own.wait()


def seq_gather(kv):
    return pl.pallas_call(
        seq_kernel,
        in_specs=[pl.BlockSpec(memory_space=SEQ_SPACE)],
        out_specs=pl.BlockSpec(memory_space=SEQ_SPACE),
        out_shape=jax.ShapeDtypeStruct((32,) + kv.shape, kv.dtype),
        scratch_shapes=[
            pltpu.SemaphoreType.DMA,
            pltpu.SemaphoreType.DMA((46,)),
            pltpu.SemaphoreType.DMA((6,)),
            pltpu.SemaphoreType.DMA((24,)),
            pltpu.SemaphoreType.DMA((16,)),
        ],
        compiler_params=pltpu.CompilerParams(collective_id=1, has_side_effects=True),
        name="seq_gather",
    )(kv)


def attend_kernel(lists, counts, q_ref, kv_hbm, out_ref, kv, sems):
    tiles = q_ref.shape[0] // TILE

    def fetch(i, j):
        return pltpu.make_async_copy(kv_hbm.at[lists[i, j]], kv.at[i, pl.ds(j * TILE, TILE)], sems.at[i])

    for i in range(tiles):
        for j in range(MAXB):
            fetch(i, j).start()

    def one_tile(i, carry):
        for j in range(MAXB):
            fetch(i, j).wait()
        rows = pl.ds(pl.multiple_of(i * TILE, TILE), TILE)

        def over(width):
            keys = kv[i, : width * TILE]
            scores = lax.dot_general(
                keys, q_ref[rows, :], (((1,), (1,)), ((), ())), preferred_element_type=jnp.float32
            )
            place = lax.broadcasted_iota(jnp.int32, scores.shape, 0)
            scores = jnp.where(place < counts[i] * TILE, scores * HD ** (-0.5), -1e30)
            top = jnp.max(scores, axis=0, keepdims=True)
            weights = jnp.exp(scores - top)
            total = jnp.sum(weights, axis=0, keepdims=True)
            summed = lax.dot_general(
                keys, weights.astype(jnp.bfloat16), (((0,), (0,)), ((), ())), preferred_element_type=jnp.float32
            )
            out_ref[:, rows] = (summed[HD:] / total).astype(jnp.bfloat16)

        for low, high in ((0, 1), (1, 2), (2, 4), (4, 8)):
            pl.when((counts[i] > low) & (counts[i] <= high))(lambda high=high: over(high))
        return carry

    lax.fori_loop(0, tiles, one_tile, 0)


def attend(lists, counts, q, kv):
    rows = q.shape[0]
    tiles = rows // TILE
    return pl.pallas_call(
        attend_kernel,
        grid_spec=pltpu.PrefetchScalarGridSpec(
            num_scalar_prefetch=2,
            grid=(1,),
            in_specs=[
                pl.BlockSpec((rows, 2 * HD), lambda i, *_: (0, 0)),
                pl.BlockSpec(memory_space=pl.ANY),
            ],
            out_specs=pl.BlockSpec((HD, rows), lambda i, *_: (0, 0)),
            scratch_shapes=[
                pltpu.VMEM((tiles, MAXB * TILE, 2 * HD), jnp.bfloat16),
                pltpu.SemaphoreType.DMA((tiles,)),
            ],
        ),
        out_shape=jax.ShapeDtypeStruct((HD, rows), jnp.bfloat16),
        name="attend",
    )(lists, counts, q, kv)


def norm_kernel(x_ref, gain_ref, out_ref):
    xf = x_ref[...].astype(jnp.float32)
    scale = lax.rsqrt(jnp.mean(xf * xf, axis=-1, keepdims=True) + 1e-05)
    out_ref[...] = (xf * scale * gain_ref[...]).astype(jnp.bfloat16)


def norm(tokens, gain):
    return pl.pallas_call(
        norm_kernel, out_shape=jax.ShapeDtypeStruct(tokens.shape, jnp.bfloat16), name="norm"
    )(tokens, gain.reshape(1, -1))


def on_device(tokens, norm_gain, w_qkv, block_lists, block_counts):
    rows, w_head = team_gather(norm(tokens, norm_gain), w_qkv)
    rows, w_head = rows.reshape(-1, rows.shape[-1]), w_head.reshape(-1, WINDOW)
    qkv = jnp.dot(rows, w_head, preferred_element_type=jnp.float32).astype(jnp.bfloat16)
    odd = lax.rem(lax.axis_index("team"), 2) == 1
    qkv = jnp.where(odd, qkv[:, HD:], qkv[:, : 3 * HD])
    q = jnp.pad(qkv[:, :HD], ((0, 0), (0, HD)))
    kv = seq_gather(qkv[:, HD:])
    return attend(block_lists, block_counts, q, kv.reshape(-1, TILE, 2 * HD)).T


def solution(mesh):
    in_specs = (P(("seq", "team"), None), P(), P("team", None), P("seq", None), P("seq"))
    out_specs = P("seq", "team")
    return jax.shard_map(
        on_device, mesh=mesh, in_specs=in_specs, out_specs=out_specs, check_vma=False
    )
```
